256 devices in a mesh: section: 8 (over z), expert: 2 (over core), tensor: 16 (over y, x).
Axes of the slice: x: 4, y: 4, z: 8, core: 2. Of those that a mesh axis runs over, the one named last changes fastest.
Arguments:
- tokens: bfloat16 [8192, 6144], P(('section', 'expert'), 'tensor'), may hold values from -6 to 6
- norm_gain: float32 [4, 6144], P(None, 'tensor'), may hold values from 0.5 to 1.5
- router: float32 [4, 6144, 8], P(None, 'tensor'), may hold values from -0.078125 to 0.078125
- w_gate: bfloat16 [8, 2, 6144, 4096], P('section', 'expert', None, 'tensor'), may hold values from -0.078125 to 0.078125
- w_up: bfloat16 [8, 2, 6144, 4096], P('section', 'expert', None, 'tensor'), may hold values from -0.078125 to 0.078125
- w_down: bfloat16 [8, 2, 4096, 6144], P('section', 'expert', 'tensor'), may hold values from -0.0625 to 0.0625
- expert_ids: int32 [2, 8192, 2], P(None, ('section', 'expert')), may hold values from 0 to 7, all different within a row
- lengths: int32 [8, 8], P(None, 'expert'), may hold values from 32 to 128
Outputs:
- encoded: bfloat16 [8192, 6144], P(('section', 'expert'), 'tensor')
The draws below stay inside these ranges and needn't reach their ends.
All inputs are finite; a program needn't handle non-finite values.
Results may differ from the reference program's by a relative error of at most 0.006.
Values may be sent and summed in bfloat16 or wider, within the bound.
A program may use at most 64 MiB of HBM per device.

```python
import jax
import jax.numpy as jnp
from jax import lax

D = 6144
E = 8
EXP_WIN = 2
FF_WIN = 8192
TOK_DEV = 512
SEQ_LEN = 128
STEPS = 2
CAP = 64
SEQ_DEV = 4
LAYERS = 4
FSPLIT = 1
HALF_W = 4096
FF_DEV = 256
TOKENS = 8192
N_SECTION = 8
N_EXPERT = 2
N_TENSOR = 16


def plant(values, key, least, largest):
    longest = values.shape.index(max(values.shape))
    spots = []
    for shift in (0, 1):
        where = [jax.random.randint(jax.random.fold_in(key, axis), (), 0, length) for axis, length in enumerate(values.shape)]
        where[longest] = (where[longest] + shift) % values.shape[longest]
        spots.append(tuple(where))
    return values.at[spots[0]].set(least).at[spots[1]].set(largest)


def block_scale(rng, extent, pieces, smallest, high):
    loudness = 1.0
    for axis_at, shards_of in pieces:
        draws = jax.random.uniform(jax.random.fold_in(jax.random.fold_in(rng, 6), axis_at), (shards_of,), jnp.float32, smallest / len(pieces), high / len(pieces))
        loudness = loudness * jnp.repeat(jnp.exp(draws), extent[axis_at] // shards_of).reshape((-1,) + (1,) * (len(extent) - 1 - axis_at))
    return loudness


def picks_of(rng, rows, count, top, lift):
    ranking = jax.random.permutation(jax.random.fold_in(rng, 1), count)
    favour = ranking
    for power in range(3):
        favour = favour * favour // count
    favour = favour * lift // count
    tickets = jax.random.randint(jax.random.fold_in(rng, 2), (rows, count), 0, 4096) + favour
    sure = jax.random.permutation(jax.random.fold_in(rng, 3), rows)[jnp.arange(count) % rows]
    tickets = jnp.where(jnp.arange(rows)[:, None] == sure[None, :], 1 << 14, tickets)
    score = tickets * count + jnp.arange(count)
    return lax.top_k(score.astype(jnp.int32), top)[1].astype(jnp.int32)


def noise(stream_key, extent, scale, most, shards=(), kind=jnp.bfloat16):
    values = jax.random.normal(stream_key, extent, jnp.float32) * scale
    if len(shards) > 0:
        values = block_scale(stream_key, extent, shards, -0.22, 0.18) * values
    return jnp.clip(values, min=-most, max=most).astype(kind)


def setup_inputs(seed: int = 0) -> dict:
    streams_of = jax.random.split(jax.random.key(seed), 9)
    tokens = noise(streams_of[0], (TOKENS, D), 1.0, 6.0, ((0, 16), (1, 16)))
    norm_gain = jnp.clip(1.0 + 0.1 * jax.random.normal(streams_of[1], (LAYERS, D), jnp.float32), 0.5, 1.5)
    router = noise(streams_of[2], (LAYERS, D, E), D ** -0.5, 0.078125, ((1, 16),), jnp.float32)
    w_gate = noise(streams_of[3], (N_SECTION, N_EXPERT, D, HALF_W), D ** -0.5, 0.078125, ((0, 8), (1, 2), (3, 16)))
    w_up = noise(streams_of[4], (N_SECTION, N_EXPERT, D, HALF_W), D ** -0.5, 0.078125, ((0, 8), (1, 2), (3, 16)))
    w_down = noise(streams_of[5], (N_SECTION, N_EXPERT, HALF_W, D), FF_WIN ** -0.5, 0.0625, ((0, 8), (1, 2), (2, 16)))
    expert_ids = picks_of(streams_of[6], STEPS * TOKENS, E, 2, 2048).reshape((STEPS, TOKENS, 2))
    lengths = plant(jax.random.randint(streams_of[7], (N_SECTION, N_EXPERT * SEQ_DEV), SEQ_LEN // 4, SEQ_LEN + 1), jax.random.fold_in(streams_of[7], 1), SEQ_LEN // 4, SEQ_LEN).astype(jnp.int32)
    return {"tokens": tokens, "norm_gain": norm_gain, "router": router, "w_gate": w_gate, "w_up": w_up, "w_down": w_down, "expert_ids": expert_ids, "lengths": lengths}


norm_eps = 1e-05

def route_tables(choice_ids, seq_lens, gate_logits):
    token_count = choice_ids.shape[0]
    expert_range = jnp.arange(E, dtype=jnp.int32)
    match_ids = choice_ids[:, :, None] == expert_range[None, None, :]
    one_hot = match_ids.astype(jnp.float32)
    picked = lax.optimization_barrier(jnp.sum(gate_logits[:, None, :] * one_hot, axis=2))
    first_weight = jax.nn.sigmoid(picked[:, 0] - picked[:, 1])
    second_weight = jax.nn.sigmoid(picked[:, 1] - picked[:, 0])
    dense_gates = first_weight[:, None] * one_hot[:, 0, :] + second_weight[:, None] * one_hot[:, 1, :]
    dense_gates = dense_gates[:, :EXP_WIN]
    positions = jnp.arange(token_count, dtype=jnp.int32)
    live_rows = positions % SEQ_LEN < jnp.repeat(seq_lens, SEQ_LEN, total_repeat_length=token_count)
    named = jnp.any(match_ids, axis=1)[:, :EXP_WIN] & live_rows[:, None]
    named_int = named.astype(jnp.int32)
    earlier = jnp.cumsum(named_int, axis=0) - named_int
    slot_range = jnp.arange(CAP, dtype=jnp.int32)
    placed = named[None, :, :] & (earlier[None, :, :] == slot_range[:, None, None])
    route_table = jnp.transpose(placed.astype(jnp.float32), (2, 0, 1))
    return (route_table, route_table * jnp.transpose(dense_gates)[:, None, :])

def prepare_group(group_rows, seq_lens, choice_ids, gain_row, router_matrix):
    as_float = group_rows.astype(jnp.float32)
    inv_rms = lax.rsqrt(lax.optimization_barrier(jnp.sum(as_float * as_float, axis=1)) / D + norm_eps)
    scaled = as_float * gain_row[None, :]
    normed = (scaled * inv_rms[:, None]).astype(jnp.bfloat16)
    gate_logits = inv_rms[:, None] * jnp.dot(scaled, router_matrix, precision=lax.Precision.HIGHEST)
    route_table, weighted = route_tables(choice_ids, seq_lens, gate_logits)
    return (normed, route_table, weighted)

def expert_apply(packed):
    expert_rows, gate_cols, up_cols, down_rows = packed
    gate_val = jnp.dot(expert_rows, gate_cols, preferred_element_type=jnp.float32)
    up_val = jnp.dot(expert_rows, up_cols, preferred_element_type=jnp.float32)
    hidden = (jax.nn.silu(gate_val) * up_val).astype(jnp.bfloat16)
    row_count = hidden.shape[0]
    hidden_parts = hidden.reshape(row_count, FSPLIT, 2, N_TENSOR, FF_DEV).astype(jnp.float32)
    down_parts = down_rows.reshape(FSPLIT, 2, N_TENSOR, FF_DEV, D).astype(jnp.float32)
    partial_out = jnp.einsum('rfbtk,fbtkd->fbtrd', hidden_parts, down_parts).astype(jnp.bfloat16)
    partial_out = lax.optimization_barrier(partial_out)
    half_out = lax.optimization_barrier(jnp.sum(partial_out.astype(jnp.float32), axis=2)).astype(jnp.bfloat16)
    half_out = lax.optimization_barrier(half_out)
    slab_out = lax.optimization_barrier(jnp.sum(half_out.astype(jnp.float32), axis=1)).astype(jnp.bfloat16)
    slab_out = lax.optimization_barrier(slab_out)
    return lax.optimization_barrier(jnp.sum(slab_out.astype(jnp.float32), axis=0))

def pair_layer(packed):
    pair_rows, pair_lens, pair_ids, gain_row, router_matrix, gate_pair, up_pair, down_pair = packed

    def prepare_batch(batch_rows, batch_lens, batch_ids):
        normed, route_table, weighted = jax.vmap(prepare_group, in_axes=(0, 0, 0, None, None))(batch_rows, batch_lens, batch_ids, gain_row, router_matrix)
        gathered = jnp.einsum('gecr,grd->egcd', route_table, normed.astype(jnp.float32), precision=lax.Precision.HIGHEST).astype(jnp.bfloat16)
        return (gathered, weighted)
    gathered, weighted = jax.vmap(prepare_batch)(pair_rows, pair_lens, pair_ids)
    expert_rows = jnp.transpose(gathered, (1, 0, 2, 3, 4)).reshape(EXP_WIN, 2 * N_EXPERT * CAP, D)
    gate_cols = gate_pair.reshape(2, EXP_WIN, FSPLIT, D, HALF_W).transpose(1, 3, 2, 0, 4).reshape(EXP_WIN, D, FF_WIN)
    up_cols = up_pair.reshape(2, EXP_WIN, FSPLIT, D, HALF_W).transpose(1, 3, 2, 0, 4).reshape(EXP_WIN, D, FF_WIN)
    down_rows = down_pair.reshape(2, EXP_WIN, FSPLIT, HALF_W, D).transpose(1, 2, 0, 3, 4).reshape(EXP_WIN, FF_WIN, D)
    expert_out = lax.map(expert_apply, (expert_rows, gate_cols, up_cols, down_rows))
    expert_out = expert_out.reshape(EXP_WIN, 2, N_EXPERT, CAP, D)
    mixture = jnp.einsum('cgekr,ecgkd->cgrd', weighted, expert_out, precision=lax.Precision.HIGHEST)
    return (pair_rows.astype(jnp.float32) + mixture).astype(jnp.bfloat16)

def reference(tokens, norm_gain, router, w_gate, w_up, w_down, expert_ids, lengths):
    current = tokens.reshape(N_SECTION, N_EXPERT, TOK_DEV, D)
    section_lens = lengths.reshape(N_SECTION, N_EXPERT, SEQ_DEV)
    gate_all = w_gate.reshape(LAYERS, 2, N_EXPERT, D, HALF_W)
    up_all = w_up.reshape(LAYERS, 2, N_EXPERT, D, HALF_W)
    down_all = w_down.reshape(LAYERS, 2, N_EXPERT, HALF_W, D)
    for step_index in range(STEPS):
        step_ids = expert_ids[step_index].reshape(LAYERS, 2, N_EXPERT, TOK_DEV, 2)
        paired = lax.map(pair_layer, (current.reshape(LAYERS, 2, N_EXPERT, TOK_DEV, D), section_lens.reshape(LAYERS, 2, N_EXPERT, SEQ_DEV), step_ids, norm_gain, router, gate_all, up_all, down_all))
        current = paired.reshape(N_SECTION, N_EXPERT, TOK_DEV, D)
        if step_index + 1 < STEPS:
            current = jnp.roll(current, 2, axis=0)
            section_lens = jnp.roll(section_lens, 2, axis=0)
    return current.reshape(TOKENS, D)
```

```python
import functools

import jax
import jax.numpy as jnp
from jax import lax
from jax.experimental import pallas as pl
from jax.experimental.pallas import tpu as pltpu
from jax.sharding import PartitionSpec as P

D = 6144
E = 8
SEQ_LEN = 128
STEPS = 2
CAP = 64
NORM_EPS = 1e-05
N_SEC = 8
TOK = 512
FEAT = 384
HID = 256

MESH = pl.DeviceIdType.MESH
HIGHEST = lax.Precision.HIGHEST
F32 = jnp.float32
BF16 = jnp.bfloat16
NT = (((1,), (1,)), ((), ()))
TN = (((0,), (0,)), ((), ()))


def gray(i):
    return i + (i // 2) * (1 - 2 * (i % 2))


def kernel(
    x_ref, gain_ref, router_ref, gate_hbm, up_hbm, down_hbm, ids_ref, lens_ref, out_ref,
    w_in, w_down, tri, xc, xn, one_hot, slots, slots_in, rows_out,
    ag, acc, hid, pb, passed, landed, mixed, ring, final, back,
    stat, stat_x, stat_y, scales, scales_in,
    w_sem, ag_sem, ag_send, rs_sem, rs_send, ex_send, stat_sem, stat_send,
    scale_sem, scale_send, back_sem, back_send, tok_sem, tok_send,
):
    sec = lax.axis_index("section")
    core = lax.axis_index("expert")
    t = lax.axis_index("tensor")
    py, px = t // 4, t % 4
    par = sec % 2
    mate = sec + 1 - 2 * par
    ahead = (sec + 2) % N_SEC
    mate_ahead = (mate + 2) % N_SEC
    behind = (sec + 6) % N_SEC
    mate_behind = (mate + 6) % N_SEC
    other = 1 - core
    layer = sec // 2

    def at(dx, dy):
        return ((py + dy + 4) % 4) * 4 + (px + dx + 4) % 4

    def shard(s, cf, cq):
        return at(cf, cq) if s == 0 else at(cq, cf)

    def near(s, role, d):
        off = (d, 0) if role == s else (0, d)
        return (sec, core, at(*off))

    w_copies = [
        pltpu.make_async_copy(gate_hbm, w_in.at[:, :, pl.ds(0, HID)], w_sem.at[0]),
        pltpu.make_async_copy(up_hbm, w_in.at[:, :, pl.ds(HID, HID)], w_sem.at[1]),
        pltpu.make_async_copy(down_hbm, w_down, w_sem.at[2]),
    ]
    for c in w_copies:
        c.start()

    barrier = pltpu.get_barrier_semaphore()
    peers = [(sec, core, at(d, 0)) for d in (1, 2, 3)] + [(sec, core, at(0, d)) for d in (1, 2, 3)]
    peers.append((sec, other, t))
    for there in (mate, ahead, mate_ahead, behind, mate_behind):
        peers += [(there, 0, t), (there, 1, t)]
    for peer in peers:
        pl.semaphore_signal(barrier, inc=1, device_id=peer, device_id_type=MESH)

    xc[...] = x_ref[...]
    tri[...] = (
        lax.broadcasted_iota(jnp.int32, (TOK, TOK), 0) < lax.broadcasted_iota(jnp.int32, (TOK, TOK), 1)
    ).astype(F32).astype(BF16)
    pl.semaphore_wait(barrier, len(peers))

    def remote(src, dst, send, recv, dev):
        return pltpu.make_async_remote_copy(
            src_ref=src, dst_ref=dst, send_sem=send, recv_sem=recv, device_id=dev, device_id_type=MESH
        )

    def step(st, carry):
        first = ids_ref[st, pl.ds(0, 1), :]
        second = ids_ref[st, pl.ds(1, 1), :]
        batch = (sec + 8 - 2 * st) % N_SEC
        lane = lax.broadcasted_iota(jnp.int32, (1, SEQ_LEN), 1)
        live = jnp.concatenate(
            [(lane < lens_ref[batch, q]).astype(jnp.int32) for q in range(TOK // SEQ_LEN)], axis=1
        )
        row_id = lax.broadcasted_iota(jnp.int32, (8, TOK), 0)
        named = (
            ((first == row_id) | (second == row_id)).astype(F32)
            * live.astype(F32)
            * (row_id < 2).astype(F32)
        )
        earlier = jnp.dot(named.astype(BF16), tri[...], preferred_element_type=F32)
        slot = jnp.where((named > 0.5) & (earlier < CAP - 0.5), earlier, -1.0)
        slots[st] = slot
        spot = lax.broadcasted_iota(jnp.int32, (CAP, TOK), 0).astype(F32)
        for e in range(2):
            one_hot[pl.ds(e * CAP, CAP), :] = (slot[e : e + 1, :] == spot).astype(F32).astype(BF16)
        picks = one_hot[...]
        rows = jnp.dot(picks, xc[...], preferred_element_type=F32)
        scaled = rows * gain_ref[pl.ds(layer, 1), :]
        rows_out[st] = scaled.astype(BF16).reshape(2, CAP, FEAT)

        pltpu.make_async_copy(rows_out.at[st, core], ag.at[st, t, core, 0], ag_sem.at[st, t, core, 0]).start()
        remote(
            rows_out.at[st, other], ag.at[st, t, core, 0], ex_send.at[st], ag_sem.at[st, t, core, 0],
            (sec, other, t),
        ).start()
        for e in range(2):
            remote(
                rows_out.at[st, e], ag.at[st, t, core, 1], ex_send.at[st], ag_sem.at[st, t, core, 1],
                (mate, e, t),
            ).start()

        sub = lax.broadcasted_iota(jnp.int32, (8, 2 * CAP), 0)
        half = lax.broadcasted_iota(jnp.int32, (8, 2 * CAP), 1) // CAP
        squares = lax.dot_general(jnp.ones((8, FEAT), F32), rows * rows, NT, precision=HIGHEST, preferred_element_type=F32)
        logits = lax.dot_general(router_ref[layer], scaled, NT, precision=HIGHEST, preferred_element_type=F32)
        chosen = []
        for e in range(2):
            rest = jnp.where(first == e, second, first)
            chosen.append(
                lax.dot_general(
                    (rest == row_id).astype(F32).astype(BF16), picks, NT, preferred_element_type=F32
                )
            )
        rival = jnp.where(half == 0, chosen[0], chosen[1])
        gap = jnp.sum(logits * ((sub == half).astype(F32) - rival), axis=0, keepdims=True)
        stat[st, 0] = jnp.where(sub == 0, squares, jnp.where(sub == 1, gap, 0.0))
        for d in (1, 2, 3):
            remote(
                stat.at[st, 0], stat_x.at[st, d - 1], stat_send.at[st, d - 1], stat_sem.at[st, d - 1],
                (sec, core, at(d, 0)),
            ).start()

        @pl.when(st == 0)
        def _():
            remote(slots.at[0], slots_in, tok_send.at[0], tok_sem.at[0], (ahead, core, t)).start()
            remote(x_ref, xn, tok_send.at[1], tok_sem.at[1], (ahead, core, t)).start()

        def unit_send(s, sg, which, role, d):
            remote(
                ag.at[st, which, s, sg], ag.at[st, which, s, sg], ag_send.at[st],
                ag_sem.at[st, which, s, sg], near(s, role, d),
            ).start()

        def unit_wait(s, sg, which):
            remote(
                ag.at[st, which, s, sg], ag.at[st, which, s, sg], ag_send.at[st],
                ag_sem.at[st, which, s, sg], (sec, other, t),
            ).wait_recv()

        def across(s, sg, which):
            for d in (1, -1):
                unit_send(s, sg, which, 1, d)

        def own(sg):
            for s in range(2):
                unit_wait(s, sg, t)
            for s in range(2):
                for d in (1, -1):
                    unit_send(s, sg, t, 0, d)
            for s in range(2):
                across(s, sg, t)

        own(0)
        total = stat[st, 0]
        for d in (1, 2, 3):
            remote(
                stat.at[st, 0], stat_x.at[st, d - 1], stat_send.at[st, d - 1], stat_sem.at[st, d - 1],
                (sec, core, at(d, 0)),
            ).wait_recv()
            total = total + stat_x[st, d - 1]
        stat[st, 1] = total
        for d in (1, 2, 3):
            remote(
                stat.at[st, 1], stat_y.at[st, d - 1], stat_send.at[st, d + 2], stat_sem.at[st, d + 2],
                (sec, core, at(0, d)),
            ).start()
        own(1)
        for s in range(2):
            left, right = shard(s, -1, 0), shard(s, 1, 0)
            unit_wait(s, 0, left)
            unit_send(s, 0, left, 0, 1)
            across(s, 0, left)
            unit_wait(s, 0, right)
            across(s, 0, right)
        for d in (1, 2, 3):
            remote(
                stat.at[st, 1], stat_y.at[st, d - 1], stat_send.at[st, d + 2], stat_sem.at[st, d + 2],
                (sec, core, at(0, d)),
            ).wait_recv()
            total = total + stat_y[st, d - 1]
        inv = lax.rsqrt(total[0:1, :] / D + NORM_EPS)
        share = jax.nn.sigmoid(inv * total[1:2, :])
        scale = jnp.where(sub == 0, inv, jnp.where(sub == 1, share, 0.0))
        scales[st, 0] = scale
        scales[st, 1] = pltpu.roll(scale, CAP, 1)
        pltpu.make_async_copy(scales.at[st, core], scales_in.at[st, 0, core], scale_sem.at[st, 0, core]).start()
        remote(
            scales.at[st, other], scales_in.at[st, 0, core], scale_send.at[st], scale_sem.at[st, 0, core],
            (sec, other, t),
        ).start()
        for e in range(2):
            remote(
                scales.at[st, e], scales_in.at[st, 1, core], scale_send.at[st], scale_sem.at[st, 1, core],
                (mate, e, t),
            ).start()
        for s in range(2):
            left, right = shard(s, -1, 0), shard(s, 1, 0)
            unit_wait(s, 1, right)
            unit_send(s, 1, right, 0, -1)
            across(s, 1, right)
            unit_wait(s, 1, left)
            across(s, 1, left)
        for s in range(2):
            far = shard(s, 2, 0)
            for sg in range(2):
                unit_wait(s, sg, far)
                across(s, sg, far)

        acc[...] = jnp.zeros_like(acc)

        @pl.when(st == 0)
        def _():
            w_copies[0].wait()
            w_copies[1].wait()

        def multiply(s, which):
            acc[s] += jnp.dot(
                ag[st, which, s].reshape(2 * CAP, FEAT), w_in[which], preferred_element_type=F32
            )

        def column(i, carry):
            c = gray(i)
            for s in range(2):
                left, right = shard(s, c, -1), shard(s, c, 1)
                unit_wait(s, 0, left)
                unit_send(s, 0, left, 1, 1)
                unit_wait(s, 1, right)
                unit_send(s, 1, right, 1, -1)
            for s in range(2):
                multiply(s, shard(s, c, 0))
            for s in range(2):
                left, right = shard(s, c, -1), shard(s, c, 1)
                unit_wait(s, 1, left)
                multiply(s, left)
                unit_wait(s, 0, right)
                multiply(s, right)
            return carry

        lax.fori_loop(0, 4, column, 0)

        def far_column(i, carry):
            c = gray(i)
            for s in range(2):
                far = shard(s, c, 2)
                unit_wait(s, 0, far)
                unit_wait(s, 1, far)
                multiply(s, far)
            return carry

        lax.fori_loop(0, 4, far_column, 0)

        for sg in range(2):
            for s in range(2):
                remote(
                    scales.at[st, 0], scales_in.at[st, sg, s], scale_send.at[st], scale_sem.at[st, sg, s],
                    (sec, other, t),
                ).wait_recv()
                turned = scales_in[st, sg, s].T
                inv_col = turned[:CAP, 0:1]
                share_col = turned[:CAP, 1:2]
                part = acc[s, pl.ds(sg * CAP, CAP), :]
                gate = part[:, :HID] * inv_col
                up = part[:, HID:] * inv_col
                hidden = gate / (1.0 + jnp.exp(-gate)) * up * share_col
                hid[s, pl.ds(sg * CAP, CAP), :] = hidden.astype(BF16)

        @pl.when(st == 0)
        def _():
            w_copies[2].wait()

        def ring_send(s, k, m, src, dst, role, d):
            remote(src, dst, rs_send.at[st], rs_sem.at[st, s, k, m], near(s, role, d)).start()

        def ring_wait(s, k, m, dst):
            remote(dst, dst, rs_send.at[st], rs_sem.at[st, s, k, m], (sec, other, t)).wait_recv()

        def send_far(s, k, src, role):
            ring_send(s, k, 0, src.at[0], passed.at[st, s, k, 0], role, 1)
            ring_send(s, k, 1, src.at[1], passed.at[st, s, k, 1], role, -1)

        def send_right(s, k, src, role):
            ring_send(s, k, 2, src.at[1], landed.at[st, s, k, 0, 1], role, 1)

        def send_left(s, k, src, role):
            ring_send(s, k, 3, src.at[0], landed.at[st, s, k, 1, 0], role, -1)

        def pass_on(s, k, right_src, left_src, role):
            ring_wait(s, k, 0, passed.at[st, s, k, 0])
            mixed[st, s, k, 0] = (right_src[0].astype(F32) + passed[st, s, k, 0].astype(F32)).astype(BF16)
            ring_send(s, k, 4, mixed.at[st, s, k, 0], landed.at[st, s, k, 0, 0], role, 1)
            ring_wait(s, k, 1, passed.at[st, s, k, 1])
            mixed[st, s, k, 1] = (left_src[1].astype(F32) + passed[st, s, k, 1].astype(F32)).astype(BF16)
            ring_send(s, k, 5, mixed.at[st, s, k, 1], landed.at[st, s, k, 1, 1], role, -1)

        def finish(s, k, mine):
            ring_wait(s, k, 2, landed.at[st, s, k, 0, 1])
            ring_wait(s, k, 3, landed.at[st, s, k, 1, 0])
            ring_wait(s, k, 4, landed.at[st, s, k, 0, 0])
            ring_wait(s, k, 5, landed.at[st, s, k, 1, 1])
            return (
                mine[...].astype(F32)
                + landed[st, s, k, 0].astype(F32)
                + landed[st, s, k, 1].astype(F32)
            ).astype(BF16)

        def part_of(s, c, j, k, cj):
            which = shard(s, c, cj)
            cols = pl.ds(pl.multiple_of(which * FEAT, 128), FEAT)
            value = jnp.dot(hid[s], w_down[:, cols], preferred_element_type=F32)
            pb[st, s, k, j] = value.astype(BF16).reshape(2, CAP, FEAT)
            return pb.at[st, s, k, j]

        def wave(i, carry):
            @pl.when(i < 4)
            def _():
                c = gray(3 - i)
                for s in range(2):
                    send_far(s, i, part_of(s, c, 0, i, 2), 1)
                for s in range(2):
                    send_right(s, i, part_of(s, c, 1, i, 1), 1)
                    send_left(s, i, part_of(s, c, 2, i, -1), 1)
                for s in range(2):
                    part_of(s, c, 3, i, 0)

            @pl.when((i >= 1) & (i < 5))
            def _():
                k = i - 1
                for s in range(2):
                    pass_on(s, k, pb.at[st, s, k, 1], pb.at[st, s, k, 2], 1)

            @pl.when(i >= 2)
            def _():
                k = i - 2
                for s in range(2):
                    ring[st, s, k] = finish(s, k, pb.at[st, s, k, 3])

                @pl.when(k == 0)
                def _():
                    for s in range(2):
                        send_far(s, 4, ring.at[st, s, 0], 0)

                @pl.when(k == 1)
                def _():
                    for s in range(2):
                        send_left(s, 4, ring.at[st, s, 1], 0)

                @pl.when(k == 2)
                def _():
                    for s in range(2):
                        send_right(s, 4, ring.at[st, s, 2], 0)
                        pass_on(s, 4, ring.at[st, s, 2], ring.at[st, s, 1], 0)

            return carry

        lax.fori_loop(0, 6, wave, 0)
        for s in range(2):
            final[st, s] = finish(s, 4, ring.at[st, s, 3])

        def back_wait():
            for e in range(2):
                for b in range(2):
                    remote(
                        final.at[st, 0, 0], back.at[st, e, b], back_send.at[st], back_sem.at[st, e, b],
                        (sec, other, t),
                    ).wait_recv()

        def combined(base, table):
            slab = (back[st, :, 0].astype(F32) + back[st, :, 1].astype(F32)).astype(BF16)
            mix = lax.dot_general(
                table, slab.reshape(2 * CAP, FEAT), TN, preferred_element_type=F32
            )
            return (base.astype(F32) + mix).astype(BF16)

        @pl.when(st == 0)
        def _():
            for s in range(2):
                for sg, there in ((0, ahead), (1, mate_ahead)):
                    remote(
                        final.at[0, s, sg], back.at[0, core, par], back_send.at[0], back_sem.at[0, core, par],
                        (there, s, t),
                    ).start()
            remote(slots.at[0], slots_in, tok_send.at[0], tok_sem.at[0], (ahead, core, t)).wait_recv()
            remote(x_ref, xn, tok_send.at[1], tok_sem.at[1], (ahead, core, t)).wait_recv()
            for e in range(2):
                one_hot[pl.ds(e * CAP, CAP), :] = (
                    slots_in[e : e + 1, :] == spot
                ).astype(F32).astype(BF16)
            table = one_hot[...]
            back_wait()
            xc[...] = combined(xn[...], table)

        @pl.when(st == 1)
        def _():
            pltpu.make_async_copy(final.at[1, core, 0], back.at[1, core, par], back_sem.at[1, core, par]).start()
            remote(
                final.at[1, other, 0], back.at[1, core, par], back_send.at[1], back_sem.at[1, core, par],
                (sec, other, t),
            ).start()
            for s in range(2):
                remote(
                    final.at[1, s, 1], back.at[1, core, par], back_send.at[1], back_sem.at[1, core, par],
                    (mate, s, t),
                ).start()
            back_wait()
            out_ref[...] = combined(xc[...], one_hot[...])

        sixty = ag.at[st, pl.ds(0, 15)]
        remote(sixty, sixty, ag_send.at[st], ag_sem.at[st, 0, 0, 0], (sec, other, t)).wait_send()
        remote(sixty, sixty, rs_send.at[st], ag_sem.at[st, 0, 0, 0], (sec, other, t)).wait_send()
        three = ag.at[st, 0, 0]
        one = ag.at[st, 0, 0, 0]
        for sem in (ex_send,):
            remote(three, three, sem.at[st], ag_sem.at[st, 0, 0, 0], (sec, other, t)).wait_send()
            remote(one, one, sem.at[st], ag_sem.at[st, 0, 0, 0], (sec, other, t)).wait_send()
        tiles = stat_x.at[st]
        remote(tiles, tiles, scale_send.at[st], ag_sem.at[st, 0, 0, 0], (sec, other, t)).wait_send()
        for d in range(6):
            remote(stat.at[st, 0], stat.at[st, 0], stat_send.at[st, d], stat_sem.at[st, d], (sec, other, t)).wait_send()

        @pl.when(st == 0)
        def _():
            four = ag.at[st, 0]
            remote(four, four, back_send.at[0], ag_sem.at[st, 0, 0, 0], (sec, other, t)).wait_send()
            remote(slots.at[0], slots_in, tok_send.at[0], tok_sem.at[0], (ahead, core, t)).wait_send()
            remote(x_ref, xn, tok_send.at[1], tok_sem.at[1], (ahead, core, t)).wait_send()

        @pl.when(st == 1)
        def _():
            remote(three, three, back_send.at[1], ag_sem.at[st, 0, 0, 0], (sec, other, t)).wait_send()
            remote(one, one, back_send.at[1], ag_sem.at[st, 0, 0, 0], (sec, other, t)).wait_send()

        return carry

    lax.fori_loop(0, STEPS, step, 0)


def on_device(tokens, norm_gain, router, w_gate, w_up, w_down, expert_ids, lengths):
    vmem = pl.BlockSpec(memory_space=pltpu.VMEM)
    anywhere = pl.BlockSpec(memory_space=pl.ANY)
    unit = (CAP, FEAT)
    tile = (8, 2 * CAP)
    dma = pltpu.SemaphoreType.DMA
    return pl.pallas_call(
        kernel,
        out_shape=jax.ShapeDtypeStruct((TOK, FEAT), BF16),
        in_specs=[vmem, vmem, vmem, anywhere, anywhere, anywhere, vmem, pl.BlockSpec(memory_space=pltpu.SMEM)],
        out_specs=vmem,
        scratch_shapes=[
            pltpu.VMEM((16, FEAT, 2 * HID), BF16),
            pltpu.VMEM((HID, D), BF16),
            pltpu.VMEM((TOK, TOK), BF16),
            pltpu.VMEM((TOK, FEAT), BF16),
            pltpu.VMEM((TOK, FEAT), BF16),
            pltpu.VMEM((2 * CAP, TOK), BF16),
            pltpu.VMEM((STEPS, 8, TOK), F32),
            pltpu.VMEM((8, TOK), F32),
            pltpu.VMEM((STEPS, 2) + unit, BF16),
            pltpu.VMEM((STEPS, 16, 2, 2) + unit, BF16),
            pltpu.VMEM((2, 2 * CAP, 2 * HID), F32),
            pltpu.VMEM((2, 2 * CAP, HID), BF16),
            pltpu.VMEM((STEPS, 2, 4, 4, 2) + unit, BF16),
            pltpu.VMEM((STEPS, 2, 5, 2) + unit, BF16),
            pltpu.VMEM((STEPS, 2, 5, 2, 2) + unit, BF16),
            pltpu.VMEM((STEPS, 2, 5, 2) + unit, BF16),
            pltpu.VMEM((STEPS, 2, 4, 2) + unit, BF16),
            pltpu.VMEM((STEPS, 2, 2) + unit, BF16),
            pltpu.VMEM((STEPS, 2, 2) + unit, BF16),
            pltpu.VMEM((STEPS, 2) + tile, F32),
            pltpu.VMEM((STEPS, 3) + tile, F32),
            pltpu.VMEM((STEPS, 3) + tile, F32),
            pltpu.VMEM((STEPS, 2) + tile, F32),
            pltpu.VMEM((STEPS, 2, 2) + tile, F32),
            dma((3,)),
            dma((STEPS, 16, 2, 2)),
            dma((STEPS,)),
            dma((STEPS, 2, 5, 6)),
            dma((STEPS,)),
            dma((STEPS,)),
            dma((STEPS, 6)),
            dma((STEPS, 6)),
            dma((STEPS, 2, 2)),
            dma((STEPS,)),
            dma((STEPS, 2, 2)),
            dma((STEPS,)),
            dma((2,)),
            dma((2,)),
        ],
        compiler_params=pltpu.CompilerParams(
            collective_id=0, has_side_effects=True, vmem_limit_bytes=60 * 1024 * 1024
        ),
        name="moe_relay",
    )(
        tokens,
        norm_gain,
        jnp.transpose(router, (0, 2, 1)),
        w_gate.reshape(16, FEAT, HID),
        w_up.reshape(16, FEAT, HID),
        w_down.reshape(HID, D),
        jnp.transpose(expert_ids, (0, 2, 1)),
        lengths,
    )


def solution(mesh):
    in_specs = (
        P(("section", "expert"), "tensor"),
        P(None, "tensor"),
        P(None, "tensor", None),
        P("section", "expert", None, "tensor"),
        P("section", "expert", None, "tensor"),
        P("section", "expert", "tensor", None),
        P(None, ("section", "expert"), None),
        P(None, "expert"),
    )
    out_specs = P(("section", "expert"), "tensor")
    return jax.shard_map(
        on_device, mesh=mesh, in_specs=in_specs, out_specs=out_specs, check_vma=False
    )
```

```python
import functools

import jax
import jax.numpy as jnp
from jax import lax
from jax.experimental import pallas as pl
from jax.experimental.pallas import tpu as pltpu
from jax.sharding import PartitionSpec as P

D = 6144
E = 8
SEQ_LEN = 128
STEPS = 2
CAP = 64
NORM_EPS = 1e-05
N_SEC = 8
TOK = 512
FEAT = 384
HID = 256

MESH = pl.DeviceIdType.MESH
HIGHEST = lax.Precision.HIGHEST
F32 = jnp.float32
BF16 = jnp.bfloat16
NT = (((1,), (1,)), ((), ()))
TN = (((0,), (0,)), ((), ()))


def gray(i):
    return i + (i // 2) * (1 - 2 * (i % 2))


def kernel(
    x_ref, gain_ref, router_ref, gate_hbm, up_hbm, down_hbm, ids_ref, lens_ref, out_ref,
    w_in, w_down, tri, xc, xn, one_hot, choice, taken, slots, slots_in, rows_out,
    ag, acc, hid, pb, passed, landed, mixed, ring, final, back,
    stat, stat_x, stat_y, scales, scales_in,
    w_sem, ag_sem, ag_send, rs_sem, rs_send, ex_send, stat_sem, stat_send,
    scale_sem, scale_send, back_sem, back_send, tok_sem, tok_send,
):
    sec = lax.axis_index("section")
    core = lax.axis_index("expert")
    t = lax.axis_index("tensor")
    py, px = t // 4, t % 4
    par = sec % 2
    mate = sec + 1 - 2 * par
    ahead = (sec + 2) % N_SEC
    mate_ahead = (mate + 2) % N_SEC
    behind = (sec + 6) % N_SEC
    mate_behind = (mate + 6) % N_SEC
    other = 1 - core
    layer = sec // 2

    def at(dx, dy):
        return ((py + dy + 4) % 4) * 4 + (px + dx + 4) % 4

    def shard(s, cf, cq):
        return at(cf, cq) if s == 0 else at(cq, cf)

    def near(s, role, d):
        off = (d, 0) if role == s else (0, d)
        return (sec, core, at(*off))

    w_copies = [
        pltpu.make_async_copy(gate_hbm, w_in.at[:, :, pl.ds(0, HID)], w_sem.at[0]),
        pltpu.make_async_copy(up_hbm, w_in.at[:, :, pl.ds(HID, HID)], w_sem.at[1]),
        pltpu.make_async_copy(down_hbm, w_down, w_sem.at[2]),
    ]
    for c in w_copies:
        c.start()

    barrier = pltpu.get_barrier_semaphore()
    peers = [(sec, core, at(d, 0)) for d in (1, 2, 3)] + [(sec, core, at(0, d)) for d in (1, 2, 3)]
    peers.append((sec, other, t))
    for there in (mate, ahead, mate_ahead, behind, mate_behind):
        peers += [(there, 0, t), (there, 1, t)]
    for peer in peers:
        pl.semaphore_signal(barrier, inc=1, device_id=peer, device_id_type=MESH)

    def remote(src, dst, send, recv, dev):
        return pltpu.make_async_remote_copy(
            src_ref=src, dst_ref=dst, send_sem=send, recv_sem=recv, device_id=dev, device_id_type=MESH
        )

    sub = lax.broadcasted_iota(jnp.int32, (8, 2 * CAP), 0)
    half = lax.broadcasted_iota(jnp.int32, (8, 2 * CAP), 1) // CAP
    gain = gain_ref[pl.ds(layer, 1), :]

    def table_of(slot):
        spot = lax.broadcasted_iota(jnp.int32, (CAP, TOK), 0).astype(F32)
        parts = [(slot[e : e + 1, :] == spot).astype(F32).astype(BF16) for e in range(2)]
        return jnp.concatenate(parts, axis=0)

    def route(st):
        first = ids_ref[st, pl.ds(0, 1), :]
        second = ids_ref[st, pl.ds(1, 1), :]
        batch = (sec + 8 - 2 * st) % N_SEC
        lane = lax.broadcasted_iota(jnp.int32, (1, SEQ_LEN), 1)
        live = jnp.concatenate(
            [(lane < lens_ref[q, batch]).astype(jnp.int32) for q in range(TOK // SEQ_LEN)], axis=1
        )
        row_id = lax.broadcasted_iota(jnp.int32, (8, TOK), 0)
        named = (
            ((first == row_id) | (second == row_id)).astype(F32)
            * live.astype(F32)
            * (row_id < 2).astype(F32)
        )
        earlier = jnp.dot(named.astype(BF16), tri[...], preferred_element_type=F32)
        slot = jnp.where((named > 0.5) & (earlier < CAP - 0.5), earlier, -1.0)
        slots[st] = slot
        picks = table_of(slot)
        one_hot[st] = picks
        chosen = []
        for e in range(2):
            rest = jnp.where(first == e, second, first)
            chosen.append(
                lax.dot_general(
                    (rest == row_id).astype(F32).astype(BF16), picks, NT, preferred_element_type=F32
                )
            )
        choice[st] = (sub == half).astype(F32) - jnp.where(half == 0, chosen[0], chosen[1])

    def take_rows(st, value):
        rows = jnp.dot(one_hot[st], value, preferred_element_type=F32)
        taken[...] = rows
        rows_out[st] = (rows * gain).astype(BF16).reshape(2, CAP, FEAT)

    def measure_rows(st):
        rows = taken[...]
        squares = lax.dot_general(jnp.ones((8, FEAT), F32), rows * rows, NT, precision=HIGHEST, preferred_element_type=F32)
        logits = lax.dot_general(router_ref[layer], rows * gain, NT, precision=HIGHEST, preferred_element_type=F32)
        gap = jnp.sum(logits * choice[st], axis=0, keepdims=True)
        stat[st, 0] = jnp.where(sub == 0, squares, jnp.where(sub == 1, gap, 0.0))

    tri[...] = (
        lax.broadcasted_iota(jnp.int32, (TOK, TOK), 0) < lax.broadcasted_iota(jnp.int32, (TOK, TOK), 1)
    ).astype(F32).astype(BF16)
    route(0)
    take_rows(0, x_ref[...])
    measure_rows(0)
    pl.semaphore_wait(barrier, len(peers))

    def step(st, carry):
        remote(
            rows_out.at[st, other], ag.at[st, t, core, 0], ex_send.at[st], ag_sem.at[st, t, core, 0],
            (sec, other, t),
        ).start()
        for e in range(2):
            remote(
                rows_out.at[st, e], ag.at[st, t, core, 1], ex_send.at[st], ag_sem.at[st, t, core, 1],
                (mate, e, t),
            ).start()
        for off in ((1, 0), (-1, 0), (0, 1), (0, -1)):
            remote(
                rows_out.at[st, core], ag.at[st, t, core, 0], ag_send.at[st], ag_sem.at[st, t, core, 0],
                (sec, core, at(*off)),
            ).start()
        pltpu.make_async_copy(rows_out.at[st, core], ag.at[st, t, core, 0], ag_sem.at[st, t, core, 0]).start()

        @pl.when(st == 1)
        def _():
            measure_rows(1)

        for d in (1, 2, 3):
            remote(
                stat.at[st, 0], stat_x.at[st, d - 1], stat_send.at[st, d - 1], stat_sem.at[st, d - 1],
                (sec, core, at(d, 0)),
            ).start()

        @pl.when(st == 0)
        def _():
            remote(slots.at[0], slots_in, tok_send.at[0], tok_sem.at[0], (ahead, core, t)).start()

        def unit_send(s, sg, which, role, d):
            remote(
                ag.at[st, which, s, sg], ag.at[st, which, s, sg], ag_send.at[st],
                ag_sem.at[st, which, s, sg], near(s, role, d),
            ).start()

        def unit_wait(s, sg, which):
            remote(
                ag.at[st, which, s, sg], ag.at[st, which, s, sg], ag_send.at[st],
                ag_sem.at[st, which, s, sg], (sec, other, t),
            ).wait_recv()

        def across(s, sg, which):
            for d in (1, -1):
                unit_send(s, sg, which, 1, d)

        def own(s, sg):
            unit_wait(s, sg, t)
            for off in ((1, 0), (-1, 0), (0, 1), (0, -1)):
                remote(
                    ag.at[st, t, s, sg], ag.at[st, t, s, sg], ag_send.at[st], ag_sem.at[st, t, s, sg],
                    (sec, core, at(*off)),
                ).start()

        own(other, 0)
        total = stat[st, 0]
        for d in (1, 2, 3):
            remote(
                stat.at[st, 0], stat_x.at[st, d - 1], stat_send.at[st, d - 1], stat_sem.at[st, d - 1],
                (sec, core, at(d, 0)),
            ).wait_recv()
            total = total + stat_x[st, d - 1]
        stat[st, 1] = total
        for d in (1, 2, 3):
            remote(
                stat.at[st, 1], stat_y.at[st, d - 1], stat_send.at[st, d + 2], stat_sem.at[st, d + 2],
                (sec, core, at(0, d)),
            ).start()
        own(0, 1)
        own(1, 1)
        for s in range(2):
            left, right = shard(s, -1, 0), shard(s, 1, 0)
            unit_wait(s, 0, left)
            unit_send(s, 0, left, 0, 1)
            across(s, 0, left)
            unit_wait(s, 0, right)
            across(s, 0, right)
        for d in (1, 2, 3):
            remote(
                stat.at[st, 1], stat_y.at[st, d - 1], stat_send.at[st, d + 2], stat_sem.at[st, d + 2],
                (sec, core, at(0, d)),
            ).wait_recv()
            total = total + stat_y[st, d - 1]
        inv = lax.rsqrt(total[0:1, :] / D + NORM_EPS)
        share = jax.nn.sigmoid(inv * total[1:2, :])
        scale = jnp.where(sub == 0, inv, jnp.where(sub == 1, share, 0.0))
        scales[st, 0] = scale
        scales[st, 1] = pltpu.roll(scale, CAP, 1)
        pltpu.make_async_copy(scales.at[st, core], scales_in.at[st, 0, core], scale_sem.at[st, 0, core]).start()
        remote(
            scales.at[st, other], scales_in.at[st, 0, core], scale_send.at[st], scale_sem.at[st, 0, core],
            (sec, other, t),
        ).start()
        for e in range(2):
            remote(
                scales.at[st, e], scales_in.at[st, 1, core], scale_send.at[st], scale_sem.at[st, 1, core],
                (mate, e, t),
            ).start()
        for s in range(2):
            left, right = shard(s, -1, 0), shard(s, 1, 0)
            unit_wait(s, 1, right)
            unit_send(s, 1, right, 0, -1)
            across(s, 1, right)
            unit_wait(s, 1, left)
            across(s, 1, left)
        for s in range(2):
            far = shard(s, 2, 0)
            for sg in range(2):
                unit_wait(s, sg, far)
                across(s, sg, far)

        acc[...] = jnp.zeros_like(acc)
        unit_wait(core, 0, t)

        @pl.when(st == 0)
        def _():
            route(1)
            w_copies[0].wait()
            w_copies[1].wait()

        def multiply(s, which):
            acc[s] += jnp.dot(
                ag[st, which, s].reshape(2 * CAP, FEAT), w_in[which], preferred_element_type=F32
            )

        def column(i, carry):
            c = gray(i)
            for s in range(2):
                left, right = shard(s, c, -1), shard(s, c, 1)
                unit_wait(s, 0, left)
                unit_send(s, 0, left, 1, 1)
                unit_wait(s, 1, right)
                unit_send(s, 1, right, 1, -1)
            for s in range(2):
                multiply(s, shard(s, c, 0))
            for s in range(2):
                left, right = shard(s, c, -1), shard(s, c, 1)
                unit_wait(s, 1, left)
                multiply(s, left)
                unit_wait(s, 0, right)
                multiply(s, right)
            return carry

        lax.fori_loop(0, 4, column, 0)

        def far_column(i, carry):
            c = gray(i)
            for s in range(2):
                far = shard(s, c, 2)
                unit_wait(s, 0, far)
                unit_wait(s, 1, far)
                multiply(s, far)
            return carry

        lax.fori_loop(0, 4, far_column, 0)

        for sg in range(2):
            for s in range(2):
                remote(
                    scales.at[st, 0], scales_in.at[st, sg, s], scale_send.at[st], scale_sem.at[st, sg, s],
                    (sec, other, t),
                ).wait_recv()
                turned = scales_in[st, sg, s].T
                inv_col = turned[:CAP, 0:1]
                share_col = turned[:CAP, 1:2]
                part = acc[s, pl.ds(sg * CAP, CAP), :]
                gate = part[:, :HID] * inv_col
                up = part[:, HID:] * inv_col
                hidden = gate / (1.0 + jnp.exp(-gate)) * up * share_col
                hid[s, pl.ds(sg * CAP, CAP), :] = hidden.astype(BF16)

        @pl.when(st == 0)
        def _():
            remote(x_ref, xn, tok_send.at[1], tok_sem.at[1], (ahead, core, t)).start()
            w_copies[2].wait()

        def ring_send(s, k, m, src, dst, role, d):
            remote(src, dst, rs_send.at[st], rs_sem.at[st, s, k, m], near(s, role, d)).start()

        def ring_wait(s, k, m, dst):
            remote(dst, dst, rs_send.at[st], rs_sem.at[st, s, k, m], (sec, other, t)).wait_recv()

        def send_far(s, k, src, role):
            ring_send(s, k, 0, src.at[0], passed.at[st, s, k, 0], role, 1)
            ring_send(s, k, 1, src.at[1], passed.at[st, s, k, 1], role, -1)

        def send_right(s, k, src, role):
            ring_send(s, k, 2, src.at[1], landed.at[st, s, k, 0, 1], role, 1)

        def send_left(s, k, src, role):
            ring_send(s, k, 3, src.at[0], landed.at[st, s, k, 1, 0], role, -1)

        def pass_on(s, k, right_src, left_src, role):
            ring_wait(s, k, 0, passed.at[st, s, k, 0])
            mixed[st, s, k, 0] = (right_src[0].astype(F32) + passed[st, s, k, 0].astype(F32)).astype(BF16)
            ring_send(s, k, 4, mixed.at[st, s, k, 0], landed.at[st, s, k, 0, 0], role, 1)
            ring_wait(s, k, 1, passed.at[st, s, k, 1])
            mixed[st, s, k, 1] = (left_src[1].astype(F32) + passed[st, s, k, 1].astype(F32)).astype(BF16)
            ring_send(s, k, 5, mixed.at[st, s, k, 1], landed.at[st, s, k, 1, 1], role, -1)

        def finish(s, k, mine):
            ring_wait(s, k, 2, landed.at[st, s, k, 0, 1])
            ring_wait(s, k, 3, landed.at[st, s, k, 1, 0])
            ring_wait(s, k, 4, landed.at[st, s, k, 0, 0])
            ring_wait(s, k, 5, landed.at[st, s, k, 1, 1])
            return (
                mine[...].astype(F32)
                + landed[st, s, k, 0].astype(F32)
                + landed[st, s, k, 1].astype(F32)
            ).astype(BF16)

        def part_of(s, c, j, k, cj):
            which = shard(s, c, cj)
            cols = pl.ds(pl.multiple_of(which * FEAT, 128), FEAT)
            value = jnp.dot(hid[s], w_down[:, cols], preferred_element_type=F32)
            pb[st, s, k, j] = value.astype(BF16).reshape(2, CAP, FEAT)
            return pb.at[st, s, k, j]

        def wave(i, carry):
            @pl.when(i < 4)
            def _():
                c = gray(3 - i)
                for s in range(2):
                    send_far(s, i, part_of(s, c, 0, i, 2), 1)
                for s in range(2):
                    send_right(s, i, part_of(s, c, 1, i, 1), 1)
                    send_left(s, i, part_of(s, c, 2, i, -1), 1)
                for s in range(2):
                    part_of(s, c, 3, i, 0)

            @pl.when((i >= 1) & (i < 5))
            def _():
                k = i - 1
                for s in range(2):
                    pass_on(s, k, pb.at[st, s, k, 1], pb.at[st, s, k, 2], 1)

            @pl.when(i >= 2)
            def _():
                k = i - 2
                for s in range(2):
                    ring[st, s, k] = finish(s, k, pb.at[st, s, k, 3])

                @pl.when(k == 0)
                def _():
                    for s in range(2):
                        send_far(s, 4, ring.at[st, s, 0], 0)

                @pl.when(k == 1)
                def _():
                    for s in range(2):
                        send_left(s, 4, ring.at[st, s, 1], 0)

                @pl.when(k == 2)
                def _():
                    for s in range(2):
                        send_right(s, 4, ring.at[st, s, 2], 0)
                        pass_on(s, 4, ring.at[st, s, 2], ring.at[st, s, 1], 0)

            return carry

        lax.fori_loop(0, 6, wave, 0)
        for s in range(2):
            final[st, s] = finish(s, 4, ring.at[st, s, 3])

        def back_wait():
            for e in range(2):
                for b in range(2):
                    remote(
                        final.at[st, 0, 0], back.at[st, e, b], back_send.at[st], back_sem.at[st, e, b],
                        (sec, other, t),
                    ).wait_recv()

        def combined(base, table):
            slab = (back[st, :, 0].astype(F32) + back[st, :, 1].astype(F32)).astype(BF16)
            mix = lax.dot_general(
                table, slab.reshape(2 * CAP, FEAT), TN, preferred_element_type=F32
            )
            return (base.astype(F32) + mix).astype(BF16)

        @pl.when(st == 0)
        def _():
            for s in range(2):
                for sg, there in ((0, ahead), (1, mate_ahead)):
                    remote(
                        final.at[0, s, sg], back.at[0, core, par], back_send.at[0], back_sem.at[0, core, par],
                        (there, s, t),
                    ).start()
            remote(slots.at[0], slots_in, tok_send.at[0], tok_sem.at[0], (ahead, core, t)).wait_recv()
            remote(x_ref, xn, tok_send.at[1], tok_sem.at[1], (ahead, core, t)).wait_recv()
            table = table_of(slots_in[...])
            back_wait()
            value = combined(xn[...], table)
            xc[...] = value
            take_rows(1, value)

        @pl.when(st == 1)
        def _():
            pltpu.make_async_copy(final.at[1, core, 0], back.at[1, core, par], back_sem.at[1, core, par]).start()
            remote(
                final.at[1, other, 0], back.at[1, core, par], back_send.at[1], back_sem.at[1, core, par],
                (sec, other, t),
            ).start()
            for s in range(2):
                remote(
                    final.at[1, s, 1], back.at[1, core, par], back_send.at[1], back_sem.at[1, core, par],
                    (mate, s, t),
                ).start()
            back_wait()
            out_ref[...] = combined(xc[...], one_hot[1])

        sixty = ag.at[st, pl.ds(0, 15)]
        remote(sixty, sixty, ag_send.at[st], ag_sem.at[st, 0, 0, 0], (sec, other, t)).wait_send()
        remote(sixty, sixty, rs_send.at[st], ag_sem.at[st, 0, 0, 0], (sec, other, t)).wait_send()
        three = ag.at[st, 0, 0]
        one = ag.at[st, 0, 0, 0]
        for sem in (ex_send,):
            remote(three, three, sem.at[st], ag_sem.at[st, 0, 0, 0], (sec, other, t)).wait_send()
            remote(one, one, sem.at[st], ag_sem.at[st, 0, 0, 0], (sec, other, t)).wait_send()
        tiles = stat_x.at[st]
        remote(tiles, tiles, scale_send.at[st], ag_sem.at[st, 0, 0, 0], (sec, other, t)).wait_send()
        for d in range(6):
            remote(stat.at[st, 0], stat.at[st, 0], stat_send.at[st, d], stat_sem.at[st, d], (sec, other, t)).wait_send()

        @pl.when(st == 0)
        def _():
            four = ag.at[st, 0]
            remote(four, four, back_send.at[0], ag_sem.at[st, 0, 0, 0], (sec, other, t)).wait_send()
            remote(slots.at[0], slots_in, tok_send.at[0], tok_sem.at[0], (ahead, core, t)).wait_send()
            remote(x_ref, xn, tok_send.at[1], tok_sem.at[1], (ahead, core, t)).wait_send()

        @pl.when(st == 1)
        def _():
            remote(three, three, back_send.at[1], ag_sem.at[st, 0, 0, 0], (sec, other, t)).wait_send()
            remote(one, one, back_send.at[1], ag_sem.at[st, 0, 0, 0], (sec, other, t)).wait_send()

        return carry

    lax.fori_loop(0, STEPS, step, 0)


def on_device(tokens, norm_gain, router, w_gate, w_up, w_down, expert_ids, lengths):
    vmem = pl.BlockSpec(memory_space=pltpu.VMEM)
    anywhere = pl.BlockSpec(memory_space=pl.ANY)
    unit = (CAP, FEAT)
    tile = (8, 2 * CAP)
    dma = pltpu.SemaphoreType.DMA
    return pl.pallas_call(
        kernel,
        out_shape=jax.ShapeDtypeStruct((TOK, FEAT), BF16),
        in_specs=[vmem, vmem, vmem, anywhere, anywhere, anywhere, vmem, pl.BlockSpec(memory_space=pltpu.SMEM)],
        out_specs=vmem,
        scratch_shapes=[
            pltpu.VMEM((16, FEAT, 2 * HID), BF16),
            pltpu.VMEM((HID, D), BF16),
            pltpu.VMEM((TOK, TOK), BF16),
            pltpu.VMEM((TOK, FEAT), BF16),
            pltpu.VMEM((TOK, FEAT), BF16),
            pltpu.VMEM((STEPS, 2 * CAP, TOK), BF16),
            pltpu.VMEM((STEPS,) + tile, F32),
            pltpu.VMEM((2 * CAP, FEAT), F32),
            pltpu.VMEM((STEPS, 8, TOK), F32),
            pltpu.VMEM((8, TOK), F32),
            pltpu.VMEM((STEPS, 2) + unit, BF16),
            pltpu.VMEM((STEPS, 16, 2, 2) + unit, BF16),
            pltpu.VMEM((2, 2 * CAP, 2 * HID), F32),
            pltpu.VMEM((2, 2 * CAP, HID), BF16),
            pltpu.VMEM((STEPS, 2, 4, 4, 2) + unit, BF16),
            pltpu.VMEM((STEPS, 2, 5, 2) + unit, BF16),
            pltpu.VMEM((STEPS, 2, 5, 2, 2) + unit, BF16),
            pltpu.VMEM((STEPS, 2, 5, 2) + unit, BF16),
            pltpu.VMEM((STEPS, 2, 4, 2) + unit, BF16),
            pltpu.VMEM((STEPS, 2, 2) + unit, BF16),
            pltpu.VMEM((STEPS, 2, 2) + unit, BF16),
            pltpu.VMEM((STEPS, 2) + tile, F32),
            pltpu.VMEM((STEPS, 3) + tile, F32),
            pltpu.VMEM((STEPS, 3) + tile, F32),
            pltpu.VMEM((STEPS, 2) + tile, F32),
            pltpu.VMEM((STEPS, 2, 2) + tile, F32),
            dma((3,)),
            dma((STEPS, 16, 2, 2)),
            dma((STEPS,)),
            dma((STEPS, 2, 5, 6)),
            dma((STEPS,)),
            dma((STEPS,)),
            dma((STEPS, 6)),
            dma((STEPS, 6)),
            dma((STEPS, 2, 2)),
            dma((STEPS,)),
            dma((STEPS, 2, 2)),
            dma((STEPS,)),
            dma((2,)),
            dma((2,)),
        ],
        compiler_params=pltpu.CompilerParams(
            collective_id=0, has_side_effects=True, vmem_limit_bytes=60 * 1024 * 1024
        ),
        name="moe_relay",
    )(
        tokens,
        norm_gain,
        jnp.transpose(router, (0, 2, 1)),
        w_gate.reshape(16, FEAT, HID),
        w_up.reshape(16, FEAT, HID),
        w_down.reshape(HID, D),
        jnp.transpose(expert_ids, (0, 2, 1)),
        jnp.transpose(lengths),
    )


def solution(mesh):
    in_specs = (
        P(("section", "expert"), "tensor"),
        P(None, "tensor"),
        P(None, "tensor", None),
        P("section", "expert", None, "tensor"),
        P("section", "expert", None, "tensor"),
        P("section", "expert", "tensor", None),
        P(None, ("section", "expert"), None),
        P(None, "expert"),
    )
    out_specs = P(("section", "expert"), "tensor")
    return jax.shard_map(
        on_device, mesh=mesh, in_specs=in_specs, out_specs=out_specs, check_vma=False
    )
```
